32 devices in a mesh: inner: 8 (over y, x, core), outer: 4 (over z).
Axes of the slice: x: 2, y: 2, z: 4, core: 2. Of those that a mesh axis runs over, the one named last changes fastest.
Arguments:
- coupling: float32 [4, 8, 36, 128, 128], P('outer', 'inner'), may hold values from -0.046875 to 0.046875
- log_diag: float32 [4, 8, 1024], P('outer', 'inner'), may hold values from -0.05 to 0.05
- pattern: int32 [8, 8], replicated, may hold values 0 or 1
- boundary: float32 [1024, 256], replicated, may hold values from -6 to 6
Outputs:
- transported: float32 [4, 8, 1024, 256], P('outer', 'inner')
The draws below stay inside these ranges and needn't reach their ends.
All inputs are finite; a program needn't handle non-finite values.
Results may differ from the reference program's by a relative error of at most 0.0003.
Values sent between devices are 32-bit elements; how exact they have to be, the bound alone decides.
A program may use at most 192 MiB of HBM per device.

```python
import jax
import jax.numpy as jnp
import numpy as np
from jax import lax

M = 1024
B = 256
TILE = 128
SEG_DEV = 1
NT = 8
NPACK = 36
SEGMENTS = 32
N_INNER = 8
N_OUTER = 4


def touch_ends(values, own_key, least, high):
    longest = values.shape.index(max(values.shape))
    spots = []
    for shift in (0, 1):
        where = [jax.random.randint(jax.random.fold_in(own_key, axis), (), 0, length) for axis, length in enumerate(values.shape)]
        where[longest] = (where[longest] + shift) % values.shape[longest]
        spots.append(tuple(where))
    return values.at[spots[0]].set(least).at[spots[1]].set(high)


def block_levels(rng, shape, cuts, smallest, largest):
    loudness = 1.0
    for dim, parts in cuts:
        heights = jax.random.uniform(jax.random.fold_in(jax.random.fold_in(rng, 6), dim), (parts,), jnp.float32, smallest / len(cuts), largest / len(cuts))
        loudness = loudness * jnp.repeat(jnp.exp(heights), shape[dim] // parts).reshape((-1,) + (1,) * (len(shape) - 1 - dim))
    return loudness


def gaussian(key, shape, width, bound, pieces=(), kind=jnp.bfloat16):
    values = width * jax.random.normal(key, shape, jnp.float32)
    if pieces:
        values = values * block_levels(key, shape, pieces, -0.22, 0.18)
    return jnp.clip(values, -bound, bound).astype(kind)


def setup_inputs(seed: int = 0) -> dict:
    key_of = jax.random.split(jax.random.key(seed), 5)
    return {
        "coupling": gaussian(key_of[0], (N_OUTER, N_INNER * SEG_DEV, NPACK, TILE, TILE), (M * SEGMENTS // 2) ** -0.5, 0.046875, ((0, 4), (1, 8)), jnp.float32),
        "log_diag": jnp.clip(jax.random.uniform(key_of[1], (N_OUTER, N_INNER * SEG_DEV, M), jnp.float32, -0.05, 0.05) * block_levels(key_of[1], (N_OUTER, N_INNER * SEG_DEV, M), ((0, 4), (1, 8)), -0.4, 0.0), -0.05, 0.05),
        "pattern": touch_ends((jax.random.randint(key_of[2], (NT, NT), 0, 2) < 1).astype(jnp.int32), jax.random.fold_in(key_of[2], 1), 0, 1),
        "boundary": gaussian(key_of[3], (M, B), 1.0, 6.0, (), jnp.float32),
    }


def tile_layout(tile_count):
    rows_list = []
    cols_list = []
    for tile_row in range(tile_count):
        for tile_col in range(tile_row + 1):
            rows_list.append(tile_row)
            cols_list.append(tile_col)
    return np.array(rows_list, dtype=np.int32), np.array(cols_list, dtype=np.int32)


def reference(coupling, log_diag, pattern, boundary):
    tile_count = M // TILE
    row_ids, col_ids = tile_layout(tile_count)
    weight = jnp.where(row_ids == col_ids, 1, pattern[row_ids, col_ids]).astype(jnp.float32)
    flat_coupling = coupling.reshape(-1, coupling.shape[2], TILE, TILE)
    flat_diag = log_diag.reshape(-1, M)

    def advance(state_now, inputs):
        tile_block, log_rates = inputs
        tile_grid = jnp.zeros((tile_count, tile_count, TILE, TILE), jnp.float32)
        tile_grid = tile_grid.at[row_ids, col_ids].set(tile_block * weight[:, None, None])
        dense_matrix = tile_grid.transpose(0, 2, 1, 3).reshape(M, M) + jnp.diag(jnp.exp(log_rates))
        updated = jnp.dot(dense_matrix, state_now, precision=lax.Precision.HIGHEST, preferred_element_type=jnp.float32)
        return updated, updated

    final_state, states = lax.scan(advance, boundary, (flat_coupling, flat_diag))
    return states.reshape(N_OUTER, N_INNER * SEG_DEV, M, B)
```

```python
import functools

import jax
import jax.numpy as jnp
from jax import lax
from jax.experimental import pallas as pl
from jax.experimental.pallas import tpu as pltpu
from jax.sharding import PartitionSpec as P

MESH = pl.DeviceIdType.MESH


def split(x):
    hi = x.astype(jnp.bfloat16)
    lo = (x - hi.astype(jnp.float32)).astype(jnp.bfloat16)
    return hi, lo


def packed(i, j):
    return i * (i + 1) // 2 + j


def dot(a, b):
    return jnp.dot(a, b, preferred_element_type=jnp.float32)


def kernel(
    n_inner, total, nt, t, nc, w,
    pattern, coupling, log_diag, boundary, out,
    own, other, own_log, other_log, lhs, rhs, scale, state, expanded, result,
    load_sem, log_sem, pair_send, pair_recv, log_send, log_recv,
    chain_send, chain_recv, fwd_send, first_sem, out_sem,
):
    me = lax.axis_index("outer") * n_inner + lax.axis_index("inner")
    odd = lax.rem(me, 2) == 1
    even = jnp.logical_not(odd)
    composed = jnp.logical_and(odd, me > 1)
    has_next = jnp.logical_or(me == 0, jnp.logical_and(odd, me + 2 < total))
    after = jnp.where(me == 0, 1, lax.rem(me + 2, total))
    partner = jnp.where(odd, me - 1, me + 1)
    before = lax.rem(me + total - 2, total)

    def at(index):
        return {"outer": index // n_inner, "inner": lax.rem(index, n_inner)}

    def rows(i):
        return pl.ds(i * t, t)

    def load_row(i):
        part = pl.ds(packed(i, 0), i + 1)
        return pltpu.make_async_copy(coupling.at[part], own.at[part], load_sem.at[i])

    def pair_row(i):
        part = pl.ds(packed(i, 0), i + 1)
        return pltpu.make_async_remote_copy(
            src_ref=coupling.at[part], dst_ref=other.at[part],
            send_sem=pair_send.at[i], recv_sem=pair_recv.at[i],
            device_id=at(partner), device_id_type=MESH,
        )

    def pair_log():
        return pltpu.make_async_remote_copy(
            src_ref=log_diag, dst_ref=other_log,
            send_sem=log_send, recv_sem=log_recv,
            device_id=at(partner), device_id_type=MESH,
        )

    def chain(i, c):
        return pltpu.make_async_remote_copy(
            src_ref=result.at[c, rows(i)], dst_ref=state.at[c, rows(i)],
            send_sem=chain_send.at[i, c], recv_sem=chain_recv.at[i, c],
            device_id=at(after), device_id_type=MESH,
        )

    def forward(i, c):
        return pltpu.make_async_remote_copy(
            src_ref=state.at[c, rows(i)], dst_ref=state.at[c, rows(i)],
            send_sem=fwd_send.at[i, c], recv_sem=chain_recv.at[i, c],
            device_id=at(partner), device_id_type=MESH,
        )

    def first(i, c):
        return pltpu.make_async_copy(
            boundary.at[rows(i), pl.ds(c * w, w)], state.at[c, rows(i)], first_sem.at[i, c]
        )

    def store(i, c):
        return pltpu.make_async_copy(
            result.at[c, rows(i)], out.at[rows(i), pl.ds(c * w, w)], out_sem.at[i, c]
        )

    for i in range(nt):
        load_row(i).start()
    pltpu.make_async_copy(log_diag, own_log, log_sem).start()

    @pl.when(me == 0)
    def _():
        for i in range(nt):
            for c in range(nc):
                first(i, c).start()

    barrier = pltpu.get_barrier_semaphore()
    pl.semaphore_signal(barrier, inc=1, device_id=at(partner), device_id_type=MESH)

    @pl.when(composed)
    def _():
        pl.semaphore_signal(barrier, inc=1, device_id=at(before), device_id_type=MESH)

    @pl.when(jnp.logical_and(odd, has_next))
    def _():
        pl.semaphore_signal(barrier, inc=1, device_id=at(after), device_id_type=MESH)

    greeted = 1 + composed.astype(jnp.int32) + jnp.logical_and(odd, has_next).astype(jnp.int32)
    pl.semaphore_wait(barrier, greeted)

    sends_pair = jnp.logical_and(even, me > 0)

    @pl.when(sends_pair)
    def _():
        pair_log().start()
        for i in range(nt):
            pair_row(i).start()

    def weight(i, j):
        return 1.0 if i == j else pattern[i, j].astype(jnp.float32)

    def put_lhs(i, j, tile):
        hi, lo = split(tile)
        lhs[rows(i), pl.ds(j * 3 * t, t)] = hi
        lhs[rows(i), pl.ds(j * 3 * t + t, t)] = hi
        lhs[rows(i), pl.ds(j * 3 * t + 2 * t, t)] = lo

    def growth(ref, i):
        return jnp.transpose(jnp.broadcast_to(jnp.exp(ref[pl.ds(i, 1), :]), (t, t)))

    pair = 2 if nt % 2 == 0 else 1
    zero = jnp.zeros((t, t), jnp.bfloat16)

    pltpu.make_async_copy(log_diag, own_log, log_sem).wait()
    for i in range(nt):
        scale[rows(i), :] = growth(own_log, i)
        load_row(i).wait()
        for j in range(i + 1):
            put_lhs(i, j, own[packed(i, j)] * weight(i, j))

    @pl.when(composed)
    def _():
        for i in range(0, nt, pair):
            for j in range(i + 1, i + pair):
                for p in range(3):
                    lhs[rows(i), pl.ds((j * 3 + p) * t, t)] = zero
                    rhs[pl.ds((i * 3 + p) * t, t), pl.ds(j * t, t)] = zero
        eye = lax.broadcasted_iota(jnp.int32, (t, t), 0) == lax.broadcasted_iota(jnp.int32, (t, t), 1)
        pair_log().wait_recv()
        for i in range(nt):
            pair_row(i).wait_recv()
            for j in range(i + 1):
                tile = other[packed(i, j)] * weight(i, j)
                if i == j:
                    grown = jnp.broadcast_to(jnp.exp(other_log[pl.ds(i, 1), :]), (t, t))
                    tile = tile + jnp.where(eye, grown, 0.0)
                hi, lo = split(tile)
                rhs[pl.ds(i * 3 * t, t), pl.ds(j * t, t)] = hi
                rhs[pl.ds(i * 3 * t + t, t), pl.ds(j * t, t)] = lo
                rhs[pl.ds(i * 3 * t + 2 * t, t), pl.ds(j * t, t)] = hi
            if i % pair == pair - 1:
                top = i - pair + 1
                for left in range(0, i + 1, pair):
                    deep = pl.ds(left * 3 * t, (i + 1 - left) * 3 * t)
                    block = dot(
                        lhs[pl.ds(top * t, pair * t), deep], rhs[deep, pl.ds(left * t, pair * t)]
                    )
                    for a in range(pair):
                        for b in range(pair):
                            r, s = top + a, left + b
                            if s <= r:
                                tile = block[a * t : (a + 1) * t, b * t : (b + 1) * t]
                                tile += scale[rows(r), :] * (other[packed(r, s)] * weight(r, s))
                                put_lhs(r, s, tile)
        for i in range(nt):
            scale[rows(i), :] = scale[rows(i), :] * growth(other_log, i)

    for i in range(nt):
        for c in range(nc):
            partial = None
            if i:
                partial = dot(lhs[rows(i), pl.ds(0, i * 3 * t)], expanded[c, pl.ds(0, i * 3 * t), :])

            @pl.when(me == 0)
            def _():
                first(i, c).wait()

            @pl.when(me > 0)
            def _():
                chain(i, c).wait_recv()

            @pl.when(composed)
            def _():
                forward(i, c).start()

            x = state[c, rows(i), :]
            hi, lo = split(x)
            piece = jnp.concatenate([hi, lo, hi], axis=0)
            expanded[c, pl.ds(i * 3 * t, 3 * t), :] = piece
            y = dot(lhs[rows(i), pl.ds(i * 3 * t, 3 * t)], piece) + scale[rows(i), :w] * x
            result[c, rows(i), :] = y if partial is None else y + partial

            @pl.when(has_next)
            def _():
                chain(i, c).start()

            store(i, c).start()

    for i in range(nt):
        for c in range(nc):
            store(i, c).wait()

            @pl.when(has_next)
            def _():
                chain(i, c).wait_send()

            @pl.when(composed)
            def _():
                forward(i, c).wait_send()

    @pl.when(sends_pair)
    def _():
        pair_log().wait_send()
        for i in range(nt):
            pair_row(i).wait_send()


def solution(mesh):
    n_inner, n_outer = mesh.shape["inner"], mesh.shape["outer"]

    def shards(coupling, log_diag, pattern, boundary):
        t = coupling.shape[-1]
        m, b = boundary.shape
        nt = m // t
        w = min(t, b)
        nc = b // w
        tiles = coupling.shape[2]
        dma = pltpu.SemaphoreType.DMA
        anywhere = pl.BlockSpec(memory_space=pl.ANY)
        result = pl.pallas_call(
            functools.partial(kernel, n_inner, n_inner * n_outer, nt, t, nc, w),
            out_shape=jax.ShapeDtypeStruct((m, b), jnp.float32),
            in_specs=[pl.BlockSpec(memory_space=pltpu.SMEM)] + [anywhere] * 3,
            out_specs=anywhere,
            scratch_shapes=[
                pltpu.VMEM((tiles, t, t), jnp.float32),
                pltpu.VMEM((tiles, t, t), jnp.float32),
                pltpu.VMEM((nt, t), jnp.float32),
                pltpu.VMEM((nt, t), jnp.float32),
                pltpu.VMEM((m, 3 * m), jnp.bfloat16),
                pltpu.VMEM((3 * m, m), jnp.bfloat16),
                pltpu.VMEM((m, t), jnp.float32),
                pltpu.VMEM((nc, m, w), jnp.float32),
                pltpu.VMEM((nc, 3 * m, w), jnp.bfloat16),
                pltpu.VMEM((nc, m, w), jnp.float32),
                dma((nt,)), dma, dma((nt,)), dma((nt,)), dma, dma,
                dma((nt, nc)), dma((nt, nc)), dma((nt, nc)), dma((nt, nc)), dma((nt, nc)),
            ],
            compiler_params=pltpu.CompilerParams(collective_id=0, has_side_effects=True),
        )(pattern, coupling[0, 0], log_diag.reshape(nt, t), boundary)
        return result[None, None]

    return jax.shard_map(
        shards,
        mesh=mesh,
        in_specs=(P("outer", "inner", None, None, None), P("outer", "inner", None), P(), P()),
        out_specs=P("outer", "inner", None, None),
        check_vma=False,
    )
```

```python
import functools

import jax
import jax.numpy as jnp
from jax import lax
from jax.experimental import pallas as pl
from jax.experimental.pallas import tpu as pltpu
from jax.sharding import PartitionSpec as P

MESH = pl.DeviceIdType.MESH
FIRST_FAST = 4


def split(x):
    hi = x.astype(jnp.bfloat16)
    lo = (x - hi.astype(jnp.float32)).astype(jnp.bfloat16)
    return hi, lo


def packed(i, j):
    return i * (i + 1) // 2 + j


def dot(a, b):
    return jnp.dot(a, b, preferred_element_type=jnp.float32)


def kernel(
    n_inner, total, nt, t, nc, w,
    pattern, coupling, log_diag, boundary, out,
    own, other, third, own_log, other_log, third_log, sum_log,
    lhs, lhs4, rhs, scale, scale4, state, expanded, result, result4,
    load_sem, log_sem, pair_send, pair_recv, log_send, log_recv,
    help_send, help_recv, sum_send, sum_recv,
    chain_send, chain_recv, fwd_send, fast_send, first_sem, out_sem,
):
    me = lax.axis_index("outer") * n_inner + lax.axis_index("inner")
    odd = lax.rem(me, 2) == 1
    even = jnp.logical_not(odd)
    composed = jnp.logical_and(odd, me > 1)
    spot, place = lax.rem(me, 4), me // 4
    in_fast_pair = jnp.logical_and(place >= FIRST_FAST, place < total // 4 - 1)
    fast = jnp.logical_and(spot == 1, in_fast_pair)
    helper = jnp.logical_and(spot == 3, in_fast_pair)
    goes_on = jnp.logical_and(odd, jnp.logical_and(me + 2 < total, jnp.logical_not(helper)))
    has_next = jnp.logical_or(me == 0, goes_on)
    after = jnp.where(me == 0, 1, lax.rem(me + 2, total))
    fast_after = lax.rem(me + 4, total)
    partner = jnp.where(odd, me - 1, me + 1)
    back = jnp.where(jnp.logical_and(spot == 1, place > FIRST_FAST), 4, 2)
    before = lax.rem(me + total - back, total)
    pair = 2 if nt % 2 == 0 else 1
    last_group = nt - pair

    def at(index):
        return {"outer": index // n_inner, "inner": lax.rem(index, n_inner)}

    def rows(i):
        return pl.ds(i * t, t)

    def load_row(i):
        part = pl.ds(packed(i, 0), i + 1)
        return pltpu.make_async_copy(coupling.at[part], own.at[part], load_sem.at[i])

    def pair_row(i):
        part = pl.ds(packed(i, 0), i + 1)
        return pltpu.make_async_remote_copy(
            src_ref=coupling.at[part], dst_ref=other.at[part],
            send_sem=pair_send.at[i], recv_sem=pair_recv.at[i],
            device_id=at(partner), device_id_type=MESH,
        )

    def pair_log():
        return pltpu.make_async_remote_copy(
            src_ref=log_diag, dst_ref=other_log,
            send_sem=log_send, recv_sem=log_recv,
            device_id=at(partner), device_id_type=MESH,
        )

    def help_rows(top):
        part = pl.ds(packed(top, 0), packed(top + pair, 0) - packed(top, 0))
        return pltpu.make_async_remote_copy(
            src_ref=own.at[part], dst_ref=third.at[part],
            send_sem=help_send.at[top // pair], recv_sem=help_recv.at[top // pair],
            device_id=at(lax.rem(me + total - 2, total)), device_id_type=MESH,
        )

    def help_log():
        return pltpu.make_async_remote_copy(
            src_ref=sum_log, dst_ref=third_log, send_sem=sum_send, recv_sem=sum_recv,
            device_id=at(lax.rem(me + total - 2, total)), device_id_type=MESH,
        )

    def fast_chain(i, c):
        return pltpu.make_async_remote_copy(
            src_ref=result4.at[c, rows(i)], dst_ref=state.at[c, rows(i)],
            send_sem=fast_send.at[i, c], recv_sem=chain_recv.at[i, c],
            device_id=at(fast_after), device_id_type=MESH,
        )

    def chain(i, c):
        return pltpu.make_async_remote_copy(
            src_ref=result.at[c, rows(i)], dst_ref=state.at[c, rows(i)],
            send_sem=chain_send.at[i, c], recv_sem=chain_recv.at[i, c],
            device_id=at(after), device_id_type=MESH,
        )

    def forward(i, c):
        return pltpu.make_async_remote_copy(
            src_ref=state.at[c, rows(i)], dst_ref=state.at[c, rows(i)],
            send_sem=fwd_send.at[i, c], recv_sem=chain_recv.at[i, c],
            device_id=at(partner), device_id_type=MESH,
        )

    def first(i, c):
        return pltpu.make_async_copy(
            boundary.at[rows(i), pl.ds(c * w, w)], state.at[c, rows(i)], first_sem.at[i, c]
        )

    def store(i, c):
        return pltpu.make_async_copy(
            result.at[c, rows(i)], out.at[rows(i), pl.ds(c * w, w)], out_sem.at[i, c]
        )

    for i in range(nt):
        load_row(i).start()
    pltpu.make_async_copy(log_diag, own_log, log_sem).start()

    @pl.when(me == 0)
    def _():
        for i in range(nt):
            for c in range(nc):
                first(i, c).start()

    def weight(i, j):
        return 1.0 if i == j else pattern[i, j].astype(jnp.float32)

    def put_lhs(buf, i, j, tile):
        hi, lo = split(tile)
        buf[rows(i), pl.ds(j * 3 * t, t)] = hi
        buf[rows(i), pl.ds(j * 3 * t + t, t)] = hi
        buf[rows(i), pl.ds(j * 3 * t + 2 * t, t)] = lo

    def put_rhs(i, j, tile):
        hi, lo = split(tile)
        rhs[pl.ds(i * 3 * t, t), pl.ds(j * t, t)] = hi
        rhs[pl.ds(i * 3 * t + t, t), pl.ds(j * t, t)] = lo
        rhs[pl.ds(i * 3 * t + 2 * t, t), pl.ds(j * t, t)] = hi

    def growth(ref, i):
        return jnp.transpose(jnp.broadcast_to(jnp.exp(ref[pl.ds(i, 1), :]), (t, t)))

    def clear(buf):
        for i in range(0, nt, pair):
            for j in range(i + 1, i + pair):
                buf[rows(i), pl.ds(j * 3 * t, 3 * t)] = jnp.zeros((t, 3 * t), jnp.bfloat16)

    def prepare(i):
        scale[rows(i), :] = growth(own_log, i)
        load_row(i).wait()
        for j in range(i + 1):
            put_lhs(lhs, i, j, own[packed(i, j)] * weight(i, j))

    def multiply(buf, top, left_scale, right, keep):
        for left in range(0, top + pair, pair):
            deep = pl.ds(left * 3 * t, (top + pair - left) * 3 * t)
            block = dot(buf[pl.ds(top * t, pair * t), deep], rhs[deep, pl.ds(left * t, pair * t)])
            for a in range(pair):
                for b in range(pair):
                    r, s = top + a, left + b
                    if s <= r:
                        tile = block[a * t : (a + 1) * t, b * t : (b + 1) * t]
                        tile += left_scale[rows(r), :] * right(r, s)
                        put_lhs(buf, r, s, tile)
                        if keep:
                            own[packed(r, s)] = tile

    eye = lax.broadcasted_iota(jnp.int32, (t, t), 0) == lax.broadcasted_iota(jnp.int32, (t, t), 1)

    def compose_start():
        clear(lhs)
        for i in range(0, nt, pair):
            for j in range(i + 1, i + pair):
                rhs[pl.ds(i * 3 * t, 3 * t), pl.ds(j * t, t)] = jnp.zeros((3 * t, t), jnp.bfloat16)
        pair_log().wait_recv()
        sum_log[...] = own_log[...] + other_log[...]

    def compose(top):
        for i in range(top, top + pair):
            pair_row(i).wait_recv()
            for j in range(i + 1):
                tile = other[packed(i, j)] * weight(i, j)
                if i == j:
                    grown = jnp.broadcast_to(jnp.exp(other_log[pl.ds(i, 1), :]), (t, t))
                    tile = tile + jnp.where(eye, grown, 0.0)
                put_rhs(i, j, tile)
        multiply(lhs, top, scale, lambda r, s: other[packed(r, s)] * weight(r, s), True)
        for i in range(top, top + pair):
            scale[rows(i), :] = scale[rows(i), :] * growth(other_log, i)

    def compose_fast(top):
        help_rows(top).wait_recv()
        for i in range(top, top + pair):
            scale4[rows(i), :] = growth(third_log, i)
            for j in range(i + 1):
                put_lhs(lhs4, i, j, third[packed(i, j)])
        multiply(lhs4, top, scale4, lambda r, s: own[packed(r, s)], False)
        for i in range(top, top + pair):
            scale4[rows(i), :] = scale4[rows(i), :] * scale[rows(i), :]

    barrier = pltpu.get_barrier_semaphore()
    pl.semaphore_signal(barrier, inc=1, device_id=at(partner), device_id_type=MESH)

    @pl.when(composed)
    def _():
        pl.semaphore_signal(barrier, inc=1, device_id=at(before), device_id_type=MESH)

    @pl.when(goes_on)
    def _():
        pl.semaphore_signal(barrier, inc=1, device_id=at(after), device_id_type=MESH)

    @pl.when(fast)
    def _():
        pl.semaphore_signal(barrier, inc=1, device_id=at(fast_after), device_id_type=MESH)

    pltpu.make_async_copy(log_diag, own_log, log_sem).wait()
    prepare(0)

    greeted = 1 + composed.astype(jnp.int32) + goes_on.astype(jnp.int32) + fast.astype(jnp.int32)
    pl.semaphore_wait(barrier, greeted)

    sends_pair = jnp.logical_and(even, me > 0)

    @pl.when(sends_pair)
    def _():
        pair_log().start()
        for i in range(nt):
            pair_row(i).start()

    @pl.when(me > 1)
    def _():
        for i in range(1, nt):
            prepare(i)

    @pl.when(composed)
    def _():
        compose_start()

        @pl.when(helper)
        def _():
            help_log().start()

    @pl.when(jnp.logical_and(composed, me != 3))
    def _():
        for top in range(0, nt, pair):
            compose(top)

            @pl.when(helper)
            def _():
                help_rows(top).start()

    @pl.when(fast)
    def _():
        clear(lhs4)
        for i in range(nt):
            for j in range(i + 1):
                tile = own[packed(i, j)]
                if i == j:
                    tile = tile + jnp.where(eye, scale[rows(i), :], 0.0)
                put_rhs(i, j, tile)
        help_log().wait_recv()
        for top in range(0, last_group, pair):
            compose_fast(top)

    @pl.when(jnp.logical_and(fast, place != FIRST_FAST))
    def _():
        compose_fast(last_group)

    for i in range(nt):
        if i:
            @pl.when(me < 2)
            def _():
                prepare(i)

        if i % pair == 0:
            @pl.when(me == 3)
            def _():
                compose(i)

        if i == last_group:
            @pl.when(jnp.logical_and(fast, place == FIRST_FAST))
            def _():
                compose_fast(i)

        for c in range(nc):
            partial = None
            if i:
                deep = pl.ds(0, i * 3 * t)

                @pl.when(fast)
                def _():
                    result4[c, rows(i), :] = dot(lhs4[rows(i), deep], expanded[c, deep, :])

                partial = dot(lhs[rows(i), deep], expanded[c, deep, :])

            @pl.when(me == 0)
            def _():
                first(i, c).wait()

            @pl.when(me > 0)
            def _():
                chain(i, c).wait_recv()

            @pl.when(composed)
            def _():
                forward(i, c).start()

            x = state[c, rows(i), :]
            hi, lo = split(x)
            piece = jnp.concatenate([hi, lo, hi], axis=0)
            expanded[c, pl.ds(i * 3 * t, 3 * t), :] = piece
            tip = pl.ds(i * 3 * t, 3 * t)

            @pl.when(fast)
            def _():
                ahead = dot(lhs4[rows(i), tip], expanded[c, tip, :])
                ahead += scale4[rows(i), :w] * state[c, rows(i), :]
                if i:
                    ahead += result4[c, rows(i), :]
                result4[c, rows(i), :] = ahead
                fast_chain(i, c).start()

            y = dot(lhs[rows(i), tip], piece) + scale[rows(i), :w] * x
            result[c, rows(i), :] = y if partial is None else y + partial

            @pl.when(has_next)
            def _():
                chain(i, c).start()

            store(i, c).start()

    for i in range(nt):
        for c in range(nc):
            store(i, c).wait()

            @pl.when(has_next)
            def _():
                chain(i, c).wait_send()

            @pl.when(composed)
            def _():
                forward(i, c).wait_send()

            @pl.when(fast)
            def _():
                fast_chain(i, c).wait_send()

    @pl.when(sends_pair)
    def _():
        pair_log().wait_send()
        for i in range(nt):
            pair_row(i).wait_send()

    @pl.when(helper)
    def _():
        help_log().wait_send()
        for top in range(0, nt, pair):
            help_rows(top).wait_send()


def solution(mesh):
    n_inner, n_outer = mesh.shape["inner"], mesh.shape["outer"]

    def shards(coupling, log_diag, pattern, boundary):
        t = coupling.shape[-1]
        m, b = boundary.shape
        nt = m // t
        w = min(t, b)
        nc = b // w
        tiles = coupling.shape[2]
        dma = pltpu.SemaphoreType.DMA
        anywhere = pl.BlockSpec(memory_space=pl.ANY)
        result = pl.pallas_call(
            functools.partial(kernel, n_inner, n_inner * n_outer, nt, t, nc, w),
            out_shape=jax.ShapeDtypeStruct((m, b), jnp.float32),
            in_specs=[pl.BlockSpec(memory_space=pltpu.SMEM)] + [anywhere] * 3,
            out_specs=anywhere,
            scratch_shapes=[
                pltpu.VMEM((tiles, t, t), jnp.float32),
                pltpu.VMEM((tiles, t, t), jnp.float32),
                pltpu.VMEM((tiles, t, t), jnp.float32),
                pltpu.VMEM((nt, t), jnp.float32),
                pltpu.VMEM((nt, t), jnp.float32),
                pltpu.VMEM((nt, t), jnp.float32),
                pltpu.VMEM((nt, t), jnp.float32),
                pltpu.VMEM((m, 3 * m), jnp.bfloat16),
                pltpu.VMEM((m, 3 * m), jnp.bfloat16),
                pltpu.VMEM((3 * m, m), jnp.bfloat16),
                pltpu.VMEM((m, t), jnp.float32),
                pltpu.VMEM((m, t), jnp.float32),
                pltpu.VMEM((nc, m, w), jnp.float32),
                pltpu.VMEM((nc, 3 * m, w), jnp.bfloat16),
                pltpu.VMEM((nc, m, w), jnp.float32),
                pltpu.VMEM((nc, m, w), jnp.float32),
                dma((nt,)), dma, dma((nt,)), dma((nt,)), dma, dma,
                dma((nt,)), dma((nt,)), dma, dma,
                dma((nt, nc)), dma((nt, nc)), dma((nt, nc)), dma((nt, nc)), dma((nt, nc)), dma((nt, nc)),
            ],
            compiler_params=pltpu.CompilerParams(collective_id=0, has_side_effects=True),
        )(pattern, coupling[0, 0], log_diag.reshape(nt, t), boundary)
        return result[None, None]

    return jax.shard_map(
        shards,
        mesh=mesh,
        in_specs=(P("outer", "inner", None, None, None), P("outer", "inner", None), P(), P()),
        out_specs=P("outer", "inner", None, None),
        check_vma=False,
    )
```

```python
import functools

import jax
import jax.numpy as jnp
from jax import lax
from jax.experimental import pallas as pl
from jax.experimental.pallas import tpu as pltpu
from jax.sharding import PartitionSpec as P

MESH = pl.DeviceIdType.MESH
FIRST_FAST = 4


def split(x):
    hi = x.astype(jnp.bfloat16)
    lo = (x - hi.astype(jnp.float32)).astype(jnp.bfloat16)
    return hi, lo


def packed(i, j):
    return i * (i + 1) // 2 + j


def dot(a, b):
    return jnp.dot(a, b, preferred_element_type=jnp.float32)


def kernel(
    n_inner, total, nt, t, nc, w,
    pattern, coupling, log_diag, boundary, out,
    own, other, third, own_log, other_log, third_log, sum_log,
    lhs, rhs, scale, state, expanded, result,
    load_sem, log_sem, pair_send, pair_recv, log_send, log_recv,
    help_send, help_recv, sum_send, sum_recv,
    chain_send, chain_recv, fwd_send, first_sem, out_sem,
):
    me = lax.axis_index("outer") * n_inner + lax.axis_index("inner")
    odd = lax.rem(me, 2) == 1
    even = jnp.logical_not(odd)
    composed = jnp.logical_and(odd, me > 1)
    spot, place = lax.rem(me, 4), me // 4
    last = total // 4 - 1

    def is_fast(index):
        return jnp.logical_and(index >= FIRST_FAST, index < last)

    fast_pair = is_fast(place)
    slow_pair = jnp.logical_not(fast_pair)
    fast = jnp.logical_and(spot == 3, fast_pair)
    helper = jnp.logical_and(spot == 1, fast_pair)
    leaves = jnp.logical_and(spot == 3, place < last)
    has_next = jnp.logical_or(jnp.logical_or(me == 0, spot == 1), leaves)
    step = jnp.where(spot == 1, jnp.where(fast_pair, 1, 2), jnp.where(is_fast(place + 1), 4, 2))
    after = jnp.where(me == 0, 1, lax.rem(me + step, total))
    partner = jnp.where(odd, me - 1, me + 1)
    target = jnp.where(fast, me - 2, partner)
    before = lax.rem(me + total - jnp.where(fast, 4, 2), total)
    other_chip = jnp.where(spot == 1, me + 2, lax.rem(me + total - 2, total))
    cross = jnp.where(spot == 1, me + 1, lax.rem(me + total - 1, total))
    enters = jnp.logical_or(fast, jnp.logical_and(spot == 1, jnp.logical_and(slow_pair, me > 1)))
    crosses = jnp.logical_and(fast_pair, jnp.logical_or(spot == 1, spot == 2))
    pair = 2 if nt % 2 == 0 else 1
    last_group = nt - pair

    def at(index):
        return {"outer": index // n_inner, "inner": lax.rem(index, n_inner)}

    def rows(i):
        return pl.ds(i * t, t)

    def load_row(i):
        part = pl.ds(packed(i, 0), i + 1)
        return pltpu.make_async_copy(coupling.at[part], own.at[part], load_sem.at[i])

    def pair_row(i):
        part = pl.ds(packed(i, 0), i + 1)
        return pltpu.make_async_remote_copy(
            src_ref=coupling.at[part], dst_ref=other.at[part],
            send_sem=pair_send.at[i], recv_sem=pair_recv.at[i],
            device_id=at(partner), device_id_type=MESH,
        )

    def pair_log():
        return pltpu.make_async_remote_copy(
            src_ref=log_diag, dst_ref=other_log,
            send_sem=log_send, recv_sem=log_recv,
            device_id=at(partner), device_id_type=MESH,
        )

    def help_rows(top):
        part = pl.ds(packed(top, 0), packed(top + pair, 0) - packed(top, 0))
        return pltpu.make_async_remote_copy(
            src_ref=own.at[part], dst_ref=third.at[part],
            send_sem=help_send.at[top // pair], recv_sem=help_recv.at[top // pair],
            device_id=at(other_chip), device_id_type=MESH,
        )

    def help_log():
        return pltpu.make_async_remote_copy(
            src_ref=sum_log, dst_ref=third_log, send_sem=sum_send, recv_sem=sum_recv,
            device_id=at(other_chip), device_id_type=MESH,
        )

    def chain(i, c):
        return pltpu.make_async_remote_copy(
            src_ref=result.at[c, rows(i)], dst_ref=state.at[c, rows(i)],
            send_sem=chain_send.at[i, c], recv_sem=chain_recv.at[i, c],
            device_id=at(after), device_id_type=MESH,
        )

    def forward(i, c):
        return pltpu.make_async_remote_copy(
            src_ref=state.at[c, rows(i)], dst_ref=state.at[c, rows(i)],
            send_sem=fwd_send.at[i, c], recv_sem=chain_recv.at[i, c],
            device_id=at(target), device_id_type=MESH,
        )

    def first(i, c):
        return pltpu.make_async_copy(
            boundary.at[rows(i), pl.ds(c * w, w)], state.at[c, rows(i)], first_sem.at[i, c]
        )

    def store(i, c):
        return pltpu.make_async_copy(
            result.at[c, rows(i)], out.at[rows(i), pl.ds(c * w, w)], out_sem.at[i, c]
        )

    for i in range(nt):
        load_row(i).start()
    pltpu.make_async_copy(log_diag, own_log, log_sem).start()

    @pl.when(me == 0)
    def _():
        for i in range(nt):
            for c in range(nc):
                first(i, c).start()

    def weight(i, j):
        return 1.0 if i == j else pattern[i, j].astype(jnp.float32)

    def put_lhs(buf, i, j, tile):
        hi, lo = split(tile)
        buf[rows(i), pl.ds(j * 3 * t, t)] = hi
        buf[rows(i), pl.ds(j * 3 * t + t, t)] = hi
        buf[rows(i), pl.ds(j * 3 * t + 2 * t, t)] = lo

    def put_rhs(i, j, tile):
        hi, lo = split(tile)
        rhs[pl.ds(i * 3 * t, t), pl.ds(j * t, t)] = hi
        rhs[pl.ds(i * 3 * t + t, t), pl.ds(j * t, t)] = lo
        rhs[pl.ds(i * 3 * t + 2 * t, t), pl.ds(j * t, t)] = hi

    def growth(ref, i):
        return jnp.transpose(jnp.broadcast_to(jnp.exp(ref[pl.ds(i, 1), :]), (t, t)))

    def clear(buf):
        for i in range(0, nt, pair):
            for j in range(i + 1, i + pair):
                buf[rows(i), pl.ds(j * 3 * t, 3 * t)] = jnp.zeros((t, 3 * t), jnp.bfloat16)

    def prepare(i):
        scale[rows(i), :] = growth(own_log, i)
        load_row(i).wait()
        for j in range(i + 1):
            put_lhs(lhs, i, j, own[packed(i, j)] * weight(i, j))

    def multiply(buf, top, left_scale, right, keep):
        for left in range(0, top + pair, pair):
            deep = pl.ds(left * 3 * t, (top + pair - left) * 3 * t)
            block = dot(buf[pl.ds(top * t, pair * t), deep], rhs[deep, pl.ds(left * t, pair * t)])
            for a in range(pair):
                for b in range(pair):
                    r, s = top + a, left + b
                    if s <= r:
                        tile = block[a * t : (a + 1) * t, b * t : (b + 1) * t]
                        tile += left_scale[rows(r), :] * right(r, s)
                        put_lhs(buf, r, s, tile)
                        if keep:
                            own[packed(r, s)] = tile

    eye = lax.broadcasted_iota(jnp.int32, (t, t), 0) == lax.broadcasted_iota(jnp.int32, (t, t), 1)

    def compose_start():
        clear(lhs)
        for i in range(0, nt, pair):
            for j in range(i + 1, i + pair):
                rhs[pl.ds(i * 3 * t, 3 * t), pl.ds(j * t, t)] = jnp.zeros((3 * t, t), jnp.bfloat16)
        pair_log().wait_recv()
        sum_log[...] = own_log[...] + other_log[...]

    def compose(top):
        for i in range(top, top + pair):
            pair_row(i).wait_recv()
            for j in range(i + 1):
                tile = other[packed(i, j)] * weight(i, j)
                if i == j:
                    grown = jnp.broadcast_to(jnp.exp(other_log[pl.ds(i, 1), :]), (t, t))
                    tile = tile + jnp.where(eye, grown, 0.0)
                put_rhs(i, j, tile)
        multiply(lhs, top, scale, lambda r, s: other[packed(r, s)] * weight(r, s), True)
        for i in range(top, top + pair):
            scale[rows(i), :] = scale[rows(i), :] * growth(other_log, i)

    def compose_fast(top):
        help_rows(top).wait_recv()
        for i in range(top, top + pair):
            grown = growth(third_log, i)
            for j in range(i + 1):
                tile = third[packed(i, j)]
                if i == j:
                    tile = tile + jnp.where(eye, grown, 0.0)
                put_rhs(i, j, tile)
        multiply(lhs, top, scale, lambda r, s: third[packed(r, s)], False)
        for i in range(top, top + pair):
            scale[rows(i), :] = scale[rows(i), :] * growth(third_log, i)

    barrier = pltpu.get_barrier_semaphore()
    pl.semaphore_signal(barrier, inc=1, device_id=at(partner), device_id_type=MESH)

    for met, whom in ((odd, other_chip), (enters, before), (leaves, after), (crosses, cross)):
        @pl.when(met)
        def _():
            pl.semaphore_signal(barrier, inc=1, device_id=at(whom), device_id_type=MESH)

    pltpu.make_async_copy(log_diag, own_log, log_sem).wait()
    prepare(0)

    greeted = 1
    for met in (odd, enters, leaves, crosses):
        greeted = greeted + met.astype(jnp.int32)
    pl.semaphore_wait(barrier, greeted)

    sends_pair = jnp.logical_and(even, me > 0)

    @pl.when(sends_pair)
    def _():
        pair_log().start()
        for i in range(nt):
            pair_row(i).start()

    @pl.when(me > 1)
    def _():
        for i in range(1, nt):
            prepare(i)

    @pl.when(composed)
    def _():
        compose_start()

        @pl.when(helper)
        def _():
            help_log().start()

    @pl.when(jnp.logical_and(composed, me != 3))
    def _():
        for top in range(0, nt, pair):
            compose(top)

            @pl.when(helper)
            def _():
                help_rows(top).start()

    @pl.when(fast)
    def _():
        help_log().wait_recv()
        for top in range(0, last_group, pair):
            compose_fast(top)

    for i in range(nt):
        if i:
            @pl.when(me < 2)
            def _():
                prepare(i)

        if i % pair == 0:
            @pl.when(me == 3)
            def _():
                compose(i)

        if i == last_group:
            @pl.when(fast)
            def _():
                compose_fast(i)

        if i:
            deep = pl.ds(0, i * 3 * t)
            partial = dot(lhs[rows(i), deep], expanded[deep, :])
            for c in range(nc):
                result[c, rows(i), :] = partial[:, c * w : (c + 1) * w]

        for c in range(nc):
            @pl.when(me == 0)
            def _():
                first(i, c).wait()

            @pl.when(me > 0)
            def _():
                chain(i, c).wait_recv()

            @pl.when(composed)
            def _():
                forward(i, c).start()

            x = state[c, rows(i), :]
            hi, lo = split(x)
            piece = jnp.concatenate([hi, lo, hi], axis=0)
            expanded[pl.ds(i * 3 * t, 3 * t), pl.ds(c * w, w)] = piece
            tip = pl.ds(i * 3 * t, 3 * t)
            y = dot(lhs[rows(i), tip], piece) + scale[rows(i), :w] * x
            if i:
                y += result[c, rows(i), :]
            result[c, rows(i), :] = y

            @pl.when(has_next)
            def _():
                chain(i, c).start()

            store(i, c).start()

    for i in range(nt):
        for c in range(nc):
            store(i, c).wait()

            @pl.when(has_next)
            def _():
                chain(i, c).wait_send()

            @pl.when(composed)
            def _():
                forward(i, c).wait_send()

    @pl.when(sends_pair)
    def _():
        pair_log().wait_send()
        for i in range(nt):
            pair_row(i).wait_send()

    @pl.when(helper)
    def _():
        help_log().wait_send()
        for top in range(0, nt, pair):
            help_rows(top).wait_send()


def solution(mesh):
    n_inner, n_outer = mesh.shape["inner"], mesh.shape["outer"]

    def shards(coupling, log_diag, pattern, boundary):
        t = coupling.shape[-1]
        m, b = boundary.shape
        nt = m // t
        w = min(t, b)
        nc = b // w
        tiles = coupling.shape[2]
        dma = pltpu.SemaphoreType.DMA
        anywhere = pl.BlockSpec(memory_space=pl.ANY)
        result = pl.pallas_call(
            functools.partial(kernel, n_inner, n_inner * n_outer, nt, t, nc, w),
            out_shape=jax.ShapeDtypeStruct((m, b), jnp.float32),
            in_specs=[pl.BlockSpec(memory_space=pltpu.SMEM)] + [anywhere] * 3,
            out_specs=anywhere,
            scratch_shapes=[
                pltpu.VMEM((tiles, t, t), jnp.float32),
                pltpu.VMEM((tiles, t, t), jnp.float32),
                pltpu.VMEM((tiles, t, t), jnp.float32),
                pltpu.VMEM((nt, t), jnp.float32),
                pltpu.VMEM((nt, t), jnp.float32),
                pltpu.VMEM((nt, t), jnp.float32),
                pltpu.VMEM((nt, t), jnp.float32),
                pltpu.VMEM((m, 3 * m), jnp.bfloat16),
                pltpu.VMEM((3 * m, m), jnp.bfloat16),
                pltpu.VMEM((m, t), jnp.float32),
                pltpu.VMEM((nc, m, w), jnp.float32),
                pltpu.VMEM((3 * m, b), jnp.bfloat16),
                pltpu.VMEM((nc, m, w), jnp.float32),
                dma((nt,)), dma, dma((nt,)), dma((nt,)), dma, dma,
                dma((nt,)), dma((nt,)), dma, dma,
                dma((nt, nc)), dma((nt, nc)), dma((nt, nc)), dma((nt, nc)), dma((nt, nc)),
            ],
            compiler_params=pltpu.CompilerParams(collective_id=0, has_side_effects=True),
        )(pattern, coupling[0, 0], log_diag.reshape(nt, t), boundary)
        return result[None, None]

    return jax.shard_map(
        shards,
        mesh=mesh,
        in_specs=(P("outer", "inner", None, None, None), P("outer", "inner", None), P(), P()),
        out_specs=P("outer", "inner", None, None),
        check_vma=False,
    )
```

```python
import functools

import jax
import jax.numpy as jnp
from jax import lax
from jax.experimental import pallas as pl
from jax.experimental.pallas import tpu as pltpu
from jax.sharding import PartitionSpec as P

MESH = pl.DeviceIdType.MESH
FIRST_FAST = 4


def split(x):
    hi = x.astype(jnp.bfloat16)
    lo = (x - hi.astype(jnp.float32)).astype(jnp.bfloat16)
    return hi, lo


def packed(i, j):
    return i * (i + 1) // 2 + j


def dot(a, b):
    return jnp.dot(a, b, preferred_element_type=jnp.float32)


def kernel(
    n_inner, total, nt, t, nc, w,
    pattern, coupling, log_diag, boundary, out,
    own, other, third, own_log, other_log, third_log, sum_log,
    lhs, rhs, scale, state, expanded, result,
    load_sem, log_sem, pair_send, pair_recv, log_send, log_recv,
    help_send, help_recv, sum_send, sum_recv,
    chain_send, chain_recv, fwd_send, first_sem, out_sem,
):
    me = lax.axis_index("outer") * n_inner + lax.axis_index("inner")
    odd = lax.rem(me, 2) == 1
    even = jnp.logical_not(odd)
    composed = jnp.logical_and(odd, me > 1)
    spot, place = lax.rem(me, 4), me // 4
    last = total // 4 - 1

    def is_fast(index):
        return jnp.logical_and(index >= FIRST_FAST, index <= last)

    fast_pair = is_fast(place)
    slow_pair = jnp.logical_not(fast_pair)
    fast = jnp.logical_and(spot == 3, fast_pair)
    helper = jnp.logical_and(spot == 1, fast_pair)
    leaves = jnp.logical_and(spot == 3, place < last)
    has_next = jnp.logical_or(jnp.logical_or(me == 0, spot == 1), leaves)
    step = jnp.where(spot == 1, jnp.where(fast_pair, 1, 2), jnp.where(is_fast(place + 1), 4, 2))
    after = jnp.where(me == 0, 1, lax.rem(me + step, total))
    partner = jnp.where(odd, me - 1, me + 1)
    target = jnp.where(fast, me - 2, partner)
    before = lax.rem(me + total - jnp.where(fast, 4, 2), total)
    other_chip = jnp.where(spot == 1, me + 2, lax.rem(me + total - 2, total))
    cross = jnp.where(spot == 1, me + 1, lax.rem(me + total - 1, total))
    enters = jnp.logical_or(fast, jnp.logical_and(spot == 1, jnp.logical_and(slow_pair, me > 1)))
    crosses = jnp.logical_and(fast_pair, jnp.logical_or(spot == 1, spot == 2))
    pair = 2 if nt % 2 == 0 else 1
    last_group = nt - pair

    def at(index):
        return {"outer": index // n_inner, "inner": lax.rem(index, n_inner)}

    def rows(i):
        return pl.ds(i * t, t)

    def load_row(i):
        part = pl.ds(packed(i, 0), i + 1)
        return pltpu.make_async_copy(coupling.at[part], own.at[part], load_sem.at[i])

    def pair_row(i):
        part = pl.ds(packed(i, 0), i + 1)
        return pltpu.make_async_remote_copy(
            src_ref=coupling.at[part], dst_ref=other.at[part],
            send_sem=pair_send.at[i], recv_sem=pair_recv.at[i],
            device_id=at(partner), device_id_type=MESH,
        )

    def pair_log():
        return pltpu.make_async_remote_copy(
            src_ref=log_diag, dst_ref=other_log,
            send_sem=log_send, recv_sem=log_recv,
            device_id=at(partner), device_id_type=MESH,
        )

    def help_rows(top):
        part = pl.ds(packed(top, 0), packed(top + pair, 0) - packed(top, 0))
        return pltpu.make_async_remote_copy(
            src_ref=own.at[part], dst_ref=third.at[part],
            send_sem=help_send.at[top // pair], recv_sem=help_recv.at[top // pair],
            device_id=at(other_chip), device_id_type=MESH,
        )

    def help_log():
        return pltpu.make_async_remote_copy(
            src_ref=sum_log, dst_ref=third_log, send_sem=sum_send, recv_sem=sum_recv,
            device_id=at(other_chip), device_id_type=MESH,
        )

    def chain(i, c):
        return pltpu.make_async_remote_copy(
            src_ref=result.at[c, rows(i)], dst_ref=state.at[c, rows(i)],
            send_sem=chain_send.at[i, c], recv_sem=chain_recv.at[i, c],
            device_id=at(after), device_id_type=MESH,
        )

    def forward(i, c):
        return pltpu.make_async_remote_copy(
            src_ref=state.at[c, rows(i)], dst_ref=state.at[c, rows(i)],
            send_sem=fwd_send.at[i, c], recv_sem=chain_recv.at[i, c],
            device_id=at(target), device_id_type=MESH,
        )

    def first(i, c):
        return pltpu.make_async_copy(
            boundary.at[rows(i), pl.ds(c * w, w)], state.at[c, rows(i)], first_sem.at[i, c]
        )

    def store(i, c):
        return pltpu.make_async_copy(
            result.at[c, rows(i)], out.at[rows(i), pl.ds(c * w, w)], out_sem.at[i, c]
        )

    for i in range(nt):
        load_row(i).start()
    pltpu.make_async_copy(log_diag, own_log, log_sem).start()

    @pl.when(me == 0)
    def _():
        for i in range(nt):
            for c in range(nc):
                first(i, c).start()

    def weight(i, j):
        return 1.0 if i == j else pattern[i, j].astype(jnp.float32)

    def put_lhs(buf, i, j, tile):
        hi, lo = split(tile)
        buf[rows(i), pl.ds(j * 3 * t, t)] = hi
        buf[rows(i), pl.ds(j * 3 * t + t, t)] = hi
        buf[rows(i), pl.ds(j * 3 * t + 2 * t, t)] = lo

    def put_rhs(i, j, tile):
        hi, lo = split(tile)
        rhs[pl.ds(i * 3 * t, t), pl.ds(j * t, t)] = hi
        rhs[pl.ds(i * 3 * t + t, t), pl.ds(j * t, t)] = lo
        rhs[pl.ds(i * 3 * t + 2 * t, t), pl.ds(j * t, t)] = hi

    def growth(ref, i):
        return jnp.transpose(jnp.broadcast_to(jnp.exp(ref[pl.ds(i, 1), :]), (t, t)))

    def clear(buf):
        for i in range(0, nt, pair):
            for j in range(i + 1, i + pair):
                buf[rows(i), pl.ds(j * 3 * t, 3 * t)] = jnp.zeros((t, 3 * t), jnp.bfloat16)

    def prepare(i):
        scale[rows(i), :] = growth(own_log, i)
        load_row(i).wait()
        for j in range(i + 1):
            put_lhs(lhs, i, j, own[packed(i, j)] * weight(i, j))

    def multiply(buf, top, left_scale, right, keep):
        for left in range(0, top + pair, pair):
            deep = pl.ds(left * 3 * t, (top + pair - left) * 3 * t)
            block = dot(buf[pl.ds(top * t, pair * t), deep], rhs[deep, pl.ds(left * t, pair * t)])
            for a in range(pair):
                for b in range(pair):
                    r, s = top + a, left + b
                    if s <= r:
                        tile = block[a * t : (a + 1) * t, b * t : (b + 1) * t]
                        tile += left_scale[rows(r), :] * right(r, s)
                        put_lhs(buf, r, s, tile)
                        if keep:
                            own[packed(r, s)] = tile

    eye = lax.broadcasted_iota(jnp.int32, (t, t), 0) == lax.broadcasted_iota(jnp.int32, (t, t), 1)

    def compose_start():
        clear(lhs)
        for i in range(0, nt, pair):
            for j in range(i + 1, i + pair):
                rhs[pl.ds(i * 3 * t, 3 * t), pl.ds(j * t, t)] = jnp.zeros((3 * t, t), jnp.bfloat16)
        pair_log().wait_recv()
        sum_log[...] = own_log[...] + other_log[...]

    def compose(top):
        for i in range(top, top + pair):
            pair_row(i).wait_recv()
            for j in range(i + 1):
                tile = other[packed(i, j)] * weight(i, j)
                if i == j:
                    grown = jnp.broadcast_to(jnp.exp(other_log[pl.ds(i, 1), :]), (t, t))
                    tile = tile + jnp.where(eye, grown, 0.0)
                put_rhs(i, j, tile)
        multiply(lhs, top, scale, lambda r, s: other[packed(r, s)] * weight(r, s), True)
        for i in range(top, top + pair):
            scale[rows(i), :] = scale[rows(i), :] * growth(other_log, i)

    def compose_fast(top):
        help_rows(top).wait_recv()
        for i in range(top, top + pair):
            grown = growth(third_log, i)
            for j in range(i + 1):
                tile = third[packed(i, j)]
                if i == j:
                    tile = tile + jnp.where(eye, grown, 0.0)
                put_rhs(i, j, tile)
        multiply(lhs, top, scale, lambda r, s: third[packed(r, s)], False)
        for i in range(top, top + pair):
            scale[rows(i), :] = scale[rows(i), :] * growth(third_log, i)

    barrier = pltpu.get_barrier_semaphore()
    pl.semaphore_signal(barrier, inc=1, device_id=at(partner), device_id_type=MESH)

    for met, whom in ((odd, other_chip), (enters, before), (leaves, after), (crosses, cross)):
        @pl.when(met)
        def _():
            pl.semaphore_signal(barrier, inc=1, device_id=at(whom), device_id_type=MESH)

    pltpu.make_async_copy(log_diag, own_log, log_sem).wait()
    prepare(0)

    greeted = 1
    for met in (odd, enters, leaves, crosses):
        greeted = greeted + met.astype(jnp.int32)
    pl.semaphore_wait(barrier, greeted)

    sends_pair = jnp.logical_and(even, me > 0)

    @pl.when(sends_pair)
    def _():
        pair_log().start()
        for i in range(nt):
            pair_row(i).start()

    @pl.when(me > 1)
    def _():
        for i in range(1, nt):
            prepare(i)

    @pl.when(composed)
    def _():
        compose_start()

        @pl.when(helper)
        def _():
            help_log().start()

    @pl.when(jnp.logical_and(composed, me != 3))
    def _():
        for top in range(0, nt, pair):
            compose(top)

            @pl.when(helper)
            def _():
                help_rows(top).start()

    @pl.when(fast)
    def _():
        help_log().wait_recv()
        for top in range(0, last_group, pair):
            compose_fast(top)

    for i in range(nt):
        if i:
            @pl.when(me < 2)
            def _():
                prepare(i)

        if i % pair == 0:
            @pl.when(me == 3)
            def _():
                compose(i)

        if i == last_group:
            @pl.when(fast)
            def _():
                compose_fast(i)

        if i:
            deep = pl.ds(0, i * 3 * t)
            partial = dot(lhs[rows(i), deep], expanded[deep, :])
            for c in range(nc):
                result[c, rows(i), :] = partial[:, c * w : (c + 1) * w]

        for c in range(nc):
            @pl.when(me == 0)
            def _():
                first(i, c).wait()

            @pl.when(me > 0)
            def _():
                chain(i, c).wait_recv()

            @pl.when(composed)
            def _():
                forward(i, c).start()

            x = state[c, rows(i), :]
            hi, lo = split(x)
            piece = jnp.concatenate([hi, lo, hi], axis=0)
            expanded[pl.ds(i * 3 * t, 3 * t), pl.ds(c * w, w)] = piece
            tip = pl.ds(i * 3 * t, 3 * t)
            y = dot(lhs[rows(i), tip], piece) + scale[rows(i), :w] * x
            if i:
                y += result[c, rows(i), :]
            result[c, rows(i), :] = y

            @pl.when(has_next)
            def _():
                chain(i, c).start()

            store(i, c).start()

    for i in range(nt):
        for c in range(nc):
            store(i, c).wait()

            @pl.when(has_next)
            def _():
                chain(i, c).wait_send()

            @pl.when(composed)
            def _():
                forward(i, c).wait_send()

    @pl.when(sends_pair)
    def _():
        pair_log().wait_send()
        for i in range(nt):
            pair_row(i).wait_send()

    @pl.when(helper)
    def _():
        help_log().wait_send()
        for top in range(0, nt, pair):
            help_rows(top).wait_send()


def solution(mesh):
    n_inner, n_outer = mesh.shape["inner"], mesh.shape["outer"]

    def shards(coupling, log_diag, pattern, boundary):
        t = coupling.shape[-1]
        m, b = boundary.shape
        nt = m // t
        w = min(t, b)
        nc = b // w
        tiles = coupling.shape[2]
        dma = pltpu.SemaphoreType.DMA
        anywhere = pl.BlockSpec(memory_space=pl.ANY)
        result = pl.pallas_call(
            functools.partial(kernel, n_inner, n_inner * n_outer, nt, t, nc, w),
            out_shape=jax.ShapeDtypeStruct((m, b), jnp.float32),
            in_specs=[pl.BlockSpec(memory_space=pltpu.SMEM)] + [anywhere] * 3,
            out_specs=anywhere,
            scratch_shapes=[
                pltpu.VMEM((tiles, t, t), jnp.float32),
                pltpu.VMEM((tiles, t, t), jnp.float32),
                pltpu.VMEM((tiles, t, t), jnp.float32),
                pltpu.VMEM((nt, t), jnp.float32),
                pltpu.VMEM((nt, t), jnp.float32),
                pltpu.VMEM((nt, t), jnp.float32),
                pltpu.VMEM((nt, t), jnp.float32),
                pltpu.VMEM((m, 3 * m), jnp.bfloat16),
                pltpu.VMEM((3 * m, m), jnp.bfloat16),
                pltpu.VMEM((m, t), jnp.float32),
                pltpu.VMEM((nc, m, w), jnp.float32),
                pltpu.VMEM((3 * m, b), jnp.bfloat16),
                pltpu.VMEM((nc, m, w), jnp.float32),
                dma((nt,)), dma, dma((nt,)), dma((nt,)), dma, dma,
                dma((nt,)), dma((nt,)), dma, dma,
                dma((nt, nc)), dma((nt, nc)), dma((nt, nc)), dma((nt, nc)), dma((nt, nc)),
            ],
            compiler_params=pltpu.CompilerParams(collective_id=0, has_side_effects=True),
        )(pattern, coupling[0, 0], log_diag.reshape(nt, t), boundary)
        return result[None, None]

    return jax.shard_map(
        shards,
        mesh=mesh,
        in_specs=(P("outer", "inner", None, None, None), P("outer", "inner", None), P(), P()),
        out_specs=P("outer", "inner", None, None),
        check_vma=False,
    )
```

```python
import functools

import jax
import jax.numpy as jnp
from jax import lax
from jax.experimental import pallas as pl
from jax.experimental.pallas import tpu as pltpu
from jax.sharding import PartitionSpec as P

MESH = pl.DeviceIdType.MESH
FIRST_FAST = 4


def split(x):
    hi = x.astype(jnp.bfloat16)
    lo = (x - hi.astype(jnp.float32)).astype(jnp.bfloat16)
    return hi, lo


def packed(i, j):
    return i * (i + 1) // 2 + j


def dot(a, b):
    return jnp.dot(a, b, preferred_element_type=jnp.float32)


def kernel(
    n_inner, total, nt, t, nc, w,
    pattern, coupling, log_diag, boundary, out,
    own, other, third, own_log, other_log, third_log, sum_log,
    lhs, rhs, scale, state, expanded, result,
    load_sem, log_sem, pair_send, pair_recv, log_send, log_recv,
    help_send, help_recv, sum_send, sum_recv,
    chain_send, chain_recv, fwd_send, beside_send, first_sem, out_sem,
):
    me = lax.axis_index("outer") * n_inner + lax.axis_index("inner")
    odd = lax.rem(me, 2) == 1
    even = jnp.logical_not(odd)
    composed = jnp.logical_and(odd, me > 1)
    spot, place = lax.rem(me, 4), me // 4
    last = total // 4 - 1

    def is_fast(index):
        return jnp.logical_and(index >= FIRST_FAST, index <= last)

    fast_pair = is_fast(place)
    slow_pair = jnp.logical_not(fast_pair)
    fast = jnp.logical_and(spot == 3, fast_pair)
    helper = jnp.logical_and(spot == 1, fast_pair)
    leaves = jnp.logical_and(spot == 3, place < last)
    beside = jnp.logical_and(spot == 2, fast_pair)
    has_next = jnp.logical_or(me == 0, jnp.logical_or(jnp.logical_and(spot == 1, slow_pair), leaves))
    step = jnp.where(spot == 1, 2, jnp.where(is_fast(place + 1), 4, 2))
    after = jnp.where(me == 0, 1, lax.rem(me + step, total))
    partner = jnp.where(odd, me - 1, me + 1)
    target = jnp.where(fast, me - 2, partner)
    before = lax.rem(me + total - jnp.where(fast, 4, 2), total)
    other_chip = jnp.where(spot == 1, me + 2, lax.rem(me + total - 2, total))
    enters = jnp.logical_or(fast, jnp.logical_and(spot == 1, jnp.logical_and(slow_pair, me > 1)))
    pair = 2 if nt % 2 == 0 else 1
    last_group = nt - pair

    def at(index):
        return {"outer": index // n_inner, "inner": lax.rem(index, n_inner)}

    def rows(i):
        return pl.ds(i * t, t)

    def load_row(i):
        part = pl.ds(packed(i, 0), i + 1)
        return pltpu.make_async_copy(coupling.at[part], own.at[part], load_sem.at[i])

    def pair_row(i):
        part = pl.ds(packed(i, 0), i + 1)
        return pltpu.make_async_remote_copy(
            src_ref=coupling.at[part], dst_ref=other.at[part],
            send_sem=pair_send.at[i], recv_sem=pair_recv.at[i],
            device_id=at(partner), device_id_type=MESH,
        )

    def pair_log():
        return pltpu.make_async_remote_copy(
            src_ref=log_diag, dst_ref=other_log,
            send_sem=log_send, recv_sem=log_recv,
            device_id=at(partner), device_id_type=MESH,
        )

    def help_rows(top):
        part = pl.ds(packed(top, 0), packed(top + pair, 0) - packed(top, 0))
        return pltpu.make_async_remote_copy(
            src_ref=own.at[part], dst_ref=third.at[part],
            send_sem=help_send.at[top // pair], recv_sem=help_recv.at[top // pair],
            device_id=at(other_chip), device_id_type=MESH,
        )

    def help_log():
        return pltpu.make_async_remote_copy(
            src_ref=sum_log, dst_ref=third_log, send_sem=sum_send, recv_sem=sum_recv,
            device_id=at(other_chip), device_id_type=MESH,
        )

    def relay_rows(top):
        part = pl.ds(packed(top, 0), packed(top + pair, 0) - packed(top, 0))
        return pltpu.make_async_remote_copy(
            src_ref=third.at[part], dst_ref=third.at[part],
            send_sem=help_send.at[top // pair], recv_sem=help_recv.at[top // pair],
            device_id=at(partner), device_id_type=MESH,
        )

    def relay_log():
        return pltpu.make_async_remote_copy(
            src_ref=third_log, dst_ref=third_log, send_sem=sum_send, recv_sem=sum_recv,
            device_id=at(partner), device_id_type=MESH,
        )

    def beside_chain(i, c):
        return pltpu.make_async_remote_copy(
            src_ref=state.at[c, rows(i)], dst_ref=state.at[c, rows(i)],
            send_sem=beside_send.at[i, c], recv_sem=chain_recv.at[i, c],
            device_id=at(partner), device_id_type=MESH,
        )

    def chain(i, c):
        return pltpu.make_async_remote_copy(
            src_ref=result.at[c, rows(i)], dst_ref=state.at[c, rows(i)],
            send_sem=chain_send.at[i, c], recv_sem=chain_recv.at[i, c],
            device_id=at(after), device_id_type=MESH,
        )

    def forward(i, c):
        return pltpu.make_async_remote_copy(
            src_ref=state.at[c, rows(i)], dst_ref=state.at[c, rows(i)],
            send_sem=fwd_send.at[i, c], recv_sem=chain_recv.at[i, c],
            device_id=at(target), device_id_type=MESH,
        )

    def first(i, c):
        return pltpu.make_async_copy(
            boundary.at[rows(i), pl.ds(c * w, w)], state.at[c, rows(i)], first_sem.at[i, c]
        )

    def store(i, c):
        return pltpu.make_async_copy(
            result.at[c, rows(i)], out.at[rows(i), pl.ds(c * w, w)], out_sem.at[i, c]
        )

    for i in range(nt):
        load_row(i).start()
    pltpu.make_async_copy(log_diag, own_log, log_sem).start()

    @pl.when(me == 0)
    def _():
        for i in range(nt):
            for c in range(nc):
                first(i, c).start()

    def weight(i, j):
        return 1.0 if i == j else pattern[i, j].astype(jnp.float32)

    def put_lhs(buf, i, j, tile):
        hi, lo = split(tile)
        buf[rows(i), pl.ds(j * 3 * t, t)] = hi
        buf[rows(i), pl.ds(j * 3 * t + t, t)] = hi
        buf[rows(i), pl.ds(j * 3 * t + 2 * t, t)] = lo

    def put_rhs(i, j, tile):
        hi, lo = split(tile)
        rhs[pl.ds(i * 3 * t, t), pl.ds(j * t, t)] = hi
        rhs[pl.ds(i * 3 * t + t, t), pl.ds(j * t, t)] = lo
        rhs[pl.ds(i * 3 * t + 2 * t, t), pl.ds(j * t, t)] = hi

    def growth(ref, i):
        return jnp.transpose(jnp.broadcast_to(jnp.exp(ref[pl.ds(i, 1), :]), (t, t)))

    def clear(buf):
        for i in range(0, nt, pair):
            for j in range(i + 1, i + pair):
                buf[rows(i), pl.ds(j * 3 * t, 3 * t)] = jnp.zeros((t, 3 * t), jnp.bfloat16)

    def prepare(i):
        scale[rows(i), :] = growth(own_log, i)
        load_row(i).wait()
        for j in range(i + 1):
            put_lhs(lhs, i, j, own[packed(i, j)] * weight(i, j))

    def multiply(buf, top, left_scale, right, keep):
        for left in range(0, top + pair, pair):
            deep = pl.ds(left * 3 * t, (top + pair - left) * 3 * t)
            block = dot(buf[pl.ds(top * t, pair * t), deep], rhs[deep, pl.ds(left * t, pair * t)])
            for a in range(pair):
                for b in range(pair):
                    r, s = top + a, left + b
                    if s <= r:
                        tile = block[a * t : (a + 1) * t, b * t : (b + 1) * t]
                        tile += left_scale[rows(r), :] * right(r, s)
                        put_lhs(buf, r, s, tile)
                        if keep:
                            own[packed(r, s)] = tile

    eye = lax.broadcasted_iota(jnp.int32, (t, t), 0) == lax.broadcasted_iota(jnp.int32, (t, t), 1)

    def clear_both():
        clear(lhs)
        for i in range(0, nt, pair):
            for j in range(i + 1, i + pair):
                rhs[pl.ds(i * 3 * t, 3 * t), pl.ds(j * t, t)] = jnp.zeros((3 * t, t), jnp.bfloat16)

    def compose_start():
        clear_both()
        pair_log().wait_recv()
        sum_log[...] = own_log[...] + other_log[...]

    def compose(top):
        for i in range(top, top + pair):
            pair_row(i).wait_recv()
            for j in range(i + 1):
                tile = other[packed(i, j)] * weight(i, j)
                if i == j:
                    grown = jnp.broadcast_to(jnp.exp(other_log[pl.ds(i, 1), :]), (t, t))
                    tile = tile + jnp.where(eye, grown, 0.0)
                put_rhs(i, j, tile)
        multiply(lhs, top, scale, lambda r, s: other[packed(r, s)] * weight(r, s), True)
        for i in range(top, top + pair):
            scale[rows(i), :] = scale[rows(i), :] * growth(other_log, i)

    def compose_fast(top):
        help_rows(top).wait_recv()

        @pl.when(fast)
        def _():
            relay_rows(top).start()

        for i in range(top, top + pair):
            grown = growth(third_log, i)
            for j in range(i + 1):
                tile = third[packed(i, j)]
                if i == j:
                    tile = tile + jnp.where(eye, grown, 0.0)
                put_rhs(i, j, tile)
        multiply(lhs, top, scale, lambda r, s: third[packed(r, s)], False)
        for i in range(top, top + pair):
            scale[rows(i), :] = scale[rows(i), :] * growth(third_log, i)

    barrier = pltpu.get_barrier_semaphore()
    pl.semaphore_signal(barrier, inc=1, device_id=at(partner), device_id_type=MESH)

    for met, whom in ((odd, other_chip), (enters, before), (leaves, after)):
        @pl.when(met)
        def _():
            pl.semaphore_signal(barrier, inc=1, device_id=at(whom), device_id_type=MESH)

    pltpu.make_async_copy(log_diag, own_log, log_sem).wait()
    prepare(0)

    greeted = 1
    for met in (odd, enters, leaves):
        greeted = greeted + met.astype(jnp.int32)
    pl.semaphore_wait(barrier, greeted)

    sends_pair = jnp.logical_and(even, me > 0)

    @pl.when(sends_pair)
    def _():
        pair_log().start()
        for i in range(nt):
            pair_row(i).start()

    @pl.when(me > 1)
    def _():
        for i in range(1, nt):
            prepare(i)

    @pl.when(composed)
    def _():
        compose_start()

        @pl.when(helper)
        def _():
            help_log().start()

    @pl.when(jnp.logical_and(composed, me != 3))
    def _():
        for top in range(0, nt, pair):
            compose(top)

            @pl.when(helper)
            def _():
                help_rows(top).start()

    @pl.when(beside)
    def _():
        clear_both()

    @pl.when(jnp.logical_or(fast, beside))
    def _():
        help_log().wait_recv()

        @pl.when(fast)
        def _():
            relay_log().start()

        for top in range(0, last_group, pair):
            compose_fast(top)

    for i in range(nt):
        if i:
            @pl.when(me < 2)
            def _():
                prepare(i)

        if i % pair == 0:
            @pl.when(me == 3)
            def _():
                compose(i)

        if i == last_group:
            @pl.when(jnp.logical_or(fast, beside))
            def _():
                compose_fast(i)

        if i:
            deep = pl.ds(0, i * 3 * t)
            partial = dot(lhs[rows(i), deep], expanded[deep, :])
            for c in range(nc):
                result[c, rows(i), :] = partial[:, c * w : (c + 1) * w]

        for c in range(nc):
            @pl.when(me == 0)
            def _():
                first(i, c).wait()

            @pl.when(me > 0)
            def _():
                chain(i, c).wait_recv()

            @pl.when(composed)
            def _():
                forward(i, c).start()

            @pl.when(fast)
            def _():
                beside_chain(i, c).start()

            x = state[c, rows(i), :]
            hi, lo = split(x)
            piece = jnp.concatenate([hi, lo, hi], axis=0)
            expanded[pl.ds(i * 3 * t, 3 * t), pl.ds(c * w, w)] = piece
            tip = pl.ds(i * 3 * t, 3 * t)
            y = dot(lhs[rows(i), tip], piece) + scale[rows(i), :w] * x
            if i:
                y += result[c, rows(i), :]
            result[c, rows(i), :] = y

            @pl.when(has_next)
            def _():
                chain(i, c).start()

            store(i, c).start()

    for i in range(nt):
        for c in range(nc):
            store(i, c).wait()

            @pl.when(has_next)
            def _():
                chain(i, c).wait_send()

            @pl.when(composed)
            def _():
                forward(i, c).wait_send()

            @pl.when(fast)
            def _():
                beside_chain(i, c).wait_send()

    @pl.when(sends_pair)
    def _():
        pair_log().wait_send()
        for i in range(nt):
            pair_row(i).wait_send()

    @pl.when(helper)
    def _():
        help_log().wait_send()
        for top in range(0, nt, pair):
            help_rows(top).wait_send()

    @pl.when(fast)
    def _():
        relay_log().wait_send()
        for top in range(0, nt, pair):
            relay_rows(top).wait_send()


def solution(mesh):
    n_inner, n_outer = mesh.shape["inner"], mesh.shape["outer"]

    def shards(coupling, log_diag, pattern, boundary):
        t = coupling.shape[-1]
        m, b = boundary.shape
        nt = m // t
        w = min(t, b)
        nc = b // w
        tiles = coupling.shape[2]
        dma = pltpu.SemaphoreType.DMA
        anywhere = pl.BlockSpec(memory_space=pl.ANY)
        result = pl.pallas_call(
            functools.partial(kernel, n_inner, n_inner * n_outer, nt, t, nc, w),
            out_shape=jax.ShapeDtypeStruct((m, b), jnp.float32),
            in_specs=[pl.BlockSpec(memory_space=pltpu.SMEM)] + [anywhere] * 3,
            out_specs=anywhere,
            scratch_shapes=[
                pltpu.VMEM((tiles, t, t), jnp.float32),
                pltpu.VMEM((tiles, t, t), jnp.float32),
                pltpu.VMEM((tiles, t, t), jnp.float32),
                pltpu.VMEM((nt, t), jnp.float32),
                pltpu.VMEM((nt, t), jnp.float32),
                pltpu.VMEM((nt, t), jnp.float32),
                pltpu.VMEM((nt, t), jnp.float32),
                pltpu.VMEM((m, 3 * m), jnp.bfloat16),
                pltpu.VMEM((3 * m, m), jnp.bfloat16),
                pltpu.VMEM((m, t), jnp.float32),
                pltpu.VMEM((nc, m, w), jnp.float32),
                pltpu.VMEM((3 * m, b), jnp.bfloat16),
                pltpu.VMEM((nc, m, w), jnp.float32),
                dma((nt,)), dma, dma((nt,)), dma((nt,)), dma, dma,
                dma((nt,)), dma((nt,)), dma, dma,
                dma((nt, nc)), dma((nt, nc)), dma((nt, nc)), dma((nt, nc)), dma((nt, nc)), dma((nt, nc)),
            ],
            compiler_params=pltpu.CompilerParams(collective_id=0, has_side_effects=True),
        )(pattern, coupling[0, 0], log_diag.reshape(nt, t), boundary)
        return result[None, None]

    return jax.shard_map(
        shards,
        mesh=mesh,
        in_specs=(P("outer", "inner", None, None, None), P("outer", "inner", None), P(), P()),
        out_specs=P("outer", "inner", None, None),
        check_vma=False,
    )
```

```python
import functools

import jax
import jax.numpy as jnp
from jax import lax
from jax.experimental import pallas as pl
from jax.experimental.pallas import tpu as pltpu
from jax.sharding import PartitionSpec as P

MESH = pl.DeviceIdType.MESH
FIRST_FAST = 3


def split(x):
    hi = x.astype(jnp.bfloat16)
    lo = (x - hi.astype(jnp.float32)).astype(jnp.bfloat16)
    return hi, lo


def packed(i, j):
    return i * (i + 1) // 2 + j


def dot(a, b):
    return jnp.dot(a, b, preferred_element_type=jnp.float32)


def kernel(
    n_inner, total, nt, t, nc, w,
    pattern, coupling, log_diag, boundary, out,
    own, other, third, own_log, other_log, third_log, sum_log,
    lhs, rhs, scale, state, expanded, result,
    load_sem, log_sem, pair_send, pair_recv, log_send, log_recv,
    help_send, help_recv, sum_send, sum_recv,
    chain_send, chain_recv, fwd_send, beside_send, first_sem, out_sem,
):
    me = lax.axis_index("outer") * n_inner + lax.axis_index("inner")
    odd = lax.rem(me, 2) == 1
    even = jnp.logical_not(odd)
    composed = jnp.logical_and(odd, me > 1)
    spot, place = lax.rem(me, 4), me // 4
    last = total // 4 - 1

    def is_fast(index):
        return jnp.logical_and(index >= FIRST_FAST, index <= last)

    fast_pair = is_fast(place)
    slow_pair = jnp.logical_not(fast_pair)
    fast = jnp.logical_and(spot == 3, fast_pair)
    helper = jnp.logical_and(spot == 1, fast_pair)
    leaves = jnp.logical_and(spot == 3, place < last)
    beside = jnp.logical_and(spot == 2, fast_pair)
    has_next = jnp.logical_or(me == 0, jnp.logical_or(jnp.logical_and(spot == 1, slow_pair), leaves))
    step = jnp.where(spot == 1, 2, jnp.where(is_fast(place + 1), 4, 2))
    after = jnp.where(me == 0, 1, lax.rem(me + step, total))
    partner = jnp.where(odd, me - 1, me + 1)
    target = jnp.where(fast, me - 2, partner)
    before = lax.rem(me + total - jnp.where(fast, 4, 2), total)
    other_chip = jnp.where(spot == 1, me + 2, lax.rem(me + total - 2, total))
    enters = jnp.logical_or(fast, jnp.logical_and(spot == 1, jnp.logical_and(slow_pair, me > 1)))
    pair = 2 if nt % 2 == 0 else 1
    last_group = nt - pair

    def at(index):
        return {"outer": index // n_inner, "inner": lax.rem(index, n_inner)}

    def rows(i):
        return pl.ds(i * t, t)

    def load_row(i):
        part = pl.ds(packed(i, 0), i + 1)
        return pltpu.make_async_copy(coupling.at[part], own.at[part], load_sem.at[i])

    def pair_row(i):
        part = pl.ds(packed(i, 0), i + 1)
        return pltpu.make_async_remote_copy(
            src_ref=coupling.at[part], dst_ref=other.at[part],
            send_sem=pair_send.at[i], recv_sem=pair_recv.at[i],
            device_id=at(partner), device_id_type=MESH,
        )

    def pair_log():
        return pltpu.make_async_remote_copy(
            src_ref=log_diag, dst_ref=other_log,
            send_sem=log_send, recv_sem=log_recv,
            device_id=at(partner), device_id_type=MESH,
        )

    def help_rows(top):
        part = pl.ds(packed(top, 0), packed(top + pair, 0) - packed(top, 0))
        return pltpu.make_async_remote_copy(
            src_ref=own.at[part], dst_ref=third.at[part],
            send_sem=help_send.at[top // pair], recv_sem=help_recv.at[top // pair],
            device_id=at(other_chip), device_id_type=MESH,
        )

    def help_log():
        return pltpu.make_async_remote_copy(
            src_ref=sum_log, dst_ref=third_log, send_sem=sum_send, recv_sem=sum_recv,
            device_id=at(other_chip), device_id_type=MESH,
        )

    def relay_rows(top):
        part = pl.ds(packed(top, 0), packed(top + pair, 0) - packed(top, 0))
        return pltpu.make_async_remote_copy(
            src_ref=third.at[part], dst_ref=third.at[part],
            send_sem=help_send.at[top // pair], recv_sem=help_recv.at[top // pair],
            device_id=at(partner), device_id_type=MESH,
        )

    def relay_log():
        return pltpu.make_async_remote_copy(
            src_ref=third_log, dst_ref=third_log, send_sem=sum_send, recv_sem=sum_recv,
            device_id=at(partner), device_id_type=MESH,
        )

    def beside_chain(i, c):
        return pltpu.make_async_remote_copy(
            src_ref=state.at[c, rows(i)], dst_ref=state.at[c, rows(i)],
            send_sem=beside_send.at[i, c], recv_sem=chain_recv.at[i, c],
            device_id=at(partner), device_id_type=MESH,
        )

    def chain(i, c):
        return pltpu.make_async_remote_copy(
            src_ref=result.at[c, rows(i)], dst_ref=state.at[c, rows(i)],
            send_sem=chain_send.at[i, c], recv_sem=chain_recv.at[i, c],
            device_id=at(after), device_id_type=MESH,
        )

    def forward(i, c):
        return pltpu.make_async_remote_copy(
            src_ref=state.at[c, rows(i)], dst_ref=state.at[c, rows(i)],
            send_sem=fwd_send.at[i, c], recv_sem=chain_recv.at[i, c],
            device_id=at(target), device_id_type=MESH,
        )

    def first(i, c):
        return pltpu.make_async_copy(
            boundary.at[rows(i), pl.ds(c * w, w)], state.at[c, rows(i)], first_sem.at[i, c]
        )

    def store(i, c):
        return pltpu.make_async_copy(
            result.at[c, rows(i)], out.at[rows(i), pl.ds(c * w, w)], out_sem.at[i, c]
        )

    for i in range(nt):
        load_row(i).start()
    pltpu.make_async_copy(log_diag, own_log, log_sem).start()

    @pl.when(me == 0)
    def _():
        for i in range(nt):
            for c in range(nc):
                first(i, c).start()

    def weight(i, j):
        return 1.0 if i == j else pattern[i, j].astype(jnp.float32)

    def put_lhs(buf, i, j, tile):
        hi, lo = split(tile)
        buf[rows(i), pl.ds(j * 3 * t, t)] = hi
        buf[rows(i), pl.ds(j * 3 * t + t, t)] = hi
        buf[rows(i), pl.ds(j * 3 * t + 2 * t, t)] = lo

    def put_rhs(i, j, tile):
        hi, lo = split(tile)
        rhs[pl.ds(i * 3 * t, t), pl.ds(j * t, t)] = hi
        rhs[pl.ds(i * 3 * t + t, t), pl.ds(j * t, t)] = lo
        rhs[pl.ds(i * 3 * t + 2 * t, t), pl.ds(j * t, t)] = hi

    def growth(ref, i):
        return jnp.transpose(jnp.broadcast_to(jnp.exp(ref[pl.ds(i, 1), :]), (t, t)))

    def clear(buf):
        for i in range(0, nt, pair):
            for j in range(i + 1, i + pair):
                buf[rows(i), pl.ds(j * 3 * t, 3 * t)] = jnp.zeros((t, 3 * t), jnp.bfloat16)

    def prepare(i):
        scale[rows(i), :] = growth(own_log, i)
        load_row(i).wait()
        for j in range(i + 1):
            put_lhs(lhs, i, j, own[packed(i, j)] * weight(i, j))

    def multiply(buf, top, left_scale, right, keep):
        for left in range(0, top + pair, pair):
            deep = pl.ds(left * 3 * t, (top + pair - left) * 3 * t)
            block = dot(buf[pl.ds(top * t, pair * t), deep], rhs[deep, pl.ds(left * t, pair * t)])
            for a in range(pair):
                for b in range(pair):
                    r, s = top + a, left + b
                    if s <= r:
                        tile = block[a * t : (a + 1) * t, b * t : (b + 1) * t]
                        tile += left_scale[rows(r), :] * right(r, s)
                        put_lhs(buf, r, s, tile)
                        if keep:
                            own[packed(r, s)] = tile

    eye = lax.broadcasted_iota(jnp.int32, (t, t), 0) == lax.broadcasted_iota(jnp.int32, (t, t), 1)

    def clear_both():
        clear(lhs)
        for i in range(0, nt, pair):
            for j in range(i + 1, i + pair):
                rhs[pl.ds(i * 3 * t, 3 * t), pl.ds(j * t, t)] = jnp.zeros((3 * t, t), jnp.bfloat16)

    def compose_start():
        clear_both()
        pair_log().wait_recv()
        sum_log[...] = own_log[...] + other_log[...]

    def compose(top):
        for i in range(top, top + pair):
            pair_row(i).wait_recv()
            for j in range(i + 1):
                tile = other[packed(i, j)] * weight(i, j)
                if i == j:
                    grown = jnp.broadcast_to(jnp.exp(other_log[pl.ds(i, 1), :]), (t, t))
                    tile = tile + jnp.where(eye, grown, 0.0)
                put_rhs(i, j, tile)
        multiply(lhs, top, scale, lambda r, s: other[packed(r, s)] * weight(r, s), True)
        for i in range(top, top + pair):
            scale[rows(i), :] = scale[rows(i), :] * growth(other_log, i)

    def compose_fast(top):
        help_rows(top).wait_recv()

        @pl.when(fast)
        def _():
            relay_rows(top).start()

        for i in range(top, top + pair):
            grown = growth(third_log, i)
            for j in range(i + 1):
                tile = third[packed(i, j)]
                if i == j:
                    tile = tile + jnp.where(eye, grown, 0.0)
                put_rhs(i, j, tile)
        multiply(lhs, top, scale, lambda r, s: third[packed(r, s)], False)
        for i in range(top, top + pair):
            scale[rows(i), :] = scale[rows(i), :] * growth(third_log, i)

    barrier = pltpu.get_barrier_semaphore()
    pl.semaphore_signal(barrier, inc=1, device_id=at(partner), device_id_type=MESH)

    for met, whom in ((odd, other_chip), (enters, before), (leaves, after)):
        @pl.when(met)
        def _():
            pl.semaphore_signal(barrier, inc=1, device_id=at(whom), device_id_type=MESH)

    pltpu.make_async_copy(log_diag, own_log, log_sem).wait()
    prepare(0)

    greeted = 1
    for met in (odd, enters, leaves):
        greeted = greeted + met.astype(jnp.int32)
    pl.semaphore_wait(barrier, greeted)

    sends_pair = jnp.logical_and(even, me > 0)

    @pl.when(sends_pair)
    def _():
        pair_log().start()
        for i in range(nt):
            pair_row(i).start()

    @pl.when(me > 1)
    def _():
        for i in range(1, nt):
            prepare(i)

    @pl.when(composed)
    def _():
        compose_start()

        @pl.when(helper)
        def _():
            help_log().start()

    @pl.when(jnp.logical_and(composed, me != 3))
    def _():
        for top in range(0, nt, pair):
            compose(top)

            @pl.when(helper)
            def _():
                help_rows(top).start()

    @pl.when(beside)
    def _():
        clear_both()

    @pl.when(jnp.logical_or(fast, beside))
    def _():
        help_log().wait_recv()

        @pl.when(fast)
        def _():
            relay_log().start()

        for top in range(0, last_group, pair):
            compose_fast(top)

    for i in range(nt):
        if i:
            @pl.when(me < 2)
            def _():
                prepare(i)

        if i % pair == 0:
            @pl.when(me == 3)
            def _():
                compose(i)

        if i == last_group:
            @pl.when(jnp.logical_or(fast, beside))
            def _():
                compose_fast(i)

        if i:
            deep = pl.ds(0, i * 3 * t)
            partial = dot(lhs[rows(i), deep], expanded[deep, :])
            for c in range(nc):
                result[c, rows(i), :] = partial[:, c * w : (c + 1) * w]

        for c in range(nc):
            @pl.when(me == 0)
            def _():
                first(i, c).wait()

            @pl.when(me > 0)
            def _():
                chain(i, c).wait_recv()

            @pl.when(composed)
            def _():
                forward(i, c).start()

            @pl.when(fast)
            def _():
                beside_chain(i, c).start()

            x = state[c, rows(i), :]
            hi, lo = split(x)
            piece = jnp.concatenate([hi, lo, hi], axis=0)
            expanded[pl.ds(i * 3 * t, 3 * t), pl.ds(c * w, w)] = piece
            tip = pl.ds(i * 3 * t, 3 * t)
            y = dot(lhs[rows(i), tip], piece) + scale[rows(i), :w] * x
            if i:
                y += result[c, rows(i), :]
            result[c, rows(i), :] = y

            @pl.when(has_next)
            def _():
                chain(i, c).start()

            store(i, c).start()

    for i in range(nt):
        for c in range(nc):
            store(i, c).wait()

            @pl.when(has_next)
            def _():
                chain(i, c).wait_send()

            @pl.when(composed)
            def _():
                forward(i, c).wait_send()

            @pl.when(fast)
            def _():
                beside_chain(i, c).wait_send()

    @pl.when(sends_pair)
    def _():
        pair_log().wait_send()
        for i in range(nt):
            pair_row(i).wait_send()

    @pl.when(helper)
    def _():
        help_log().wait_send()
        for top in range(0, nt, pair):
            help_rows(top).wait_send()

    @pl.when(fast)
    def _():
        relay_log().wait_send()
        for top in range(0, nt, pair):
            relay_rows(top).wait_send()


def solution(mesh):
    n_inner, n_outer = mesh.shape["inner"], mesh.shape["outer"]

    def shards(coupling, log_diag, pattern, boundary):
        t = coupling.shape[-1]
        m, b = boundary.shape
        nt = m // t
        w = min(t, b)
        nc = b // w
        tiles = coupling.shape[2]
        dma = pltpu.SemaphoreType.DMA
        anywhere = pl.BlockSpec(memory_space=pl.ANY)
        result = pl.pallas_call(
            functools.partial(kernel, n_inner, n_inner * n_outer, nt, t, nc, w),
            out_shape=jax.ShapeDtypeStruct((m, b), jnp.float32),
            in_specs=[pl.BlockSpec(memory_space=pltpu.SMEM)] + [anywhere] * 3,
            out_specs=anywhere,
            scratch_shapes=[
                pltpu.VMEM((tiles, t, t), jnp.float32),
                pltpu.VMEM((tiles, t, t), jnp.float32),
                pltpu.VMEM((tiles, t, t), jnp.float32),
                pltpu.VMEM((nt, t), jnp.float32),
                pltpu.VMEM((nt, t), jnp.float32),
                pltpu.VMEM((nt, t), jnp.float32),
                pltpu.VMEM((nt, t), jnp.float32),
                pltpu.VMEM((m, 3 * m), jnp.bfloat16),
                pltpu.VMEM((3 * m, m), jnp.bfloat16),
                pltpu.VMEM((m, t), jnp.float32),
                pltpu.VMEM((nc, m, w), jnp.float32),
                pltpu.VMEM((3 * m, b), jnp.bfloat16),
                pltpu.VMEM((nc, m, w), jnp.float32),
                dma((nt,)), dma, dma((nt,)), dma((nt,)), dma, dma,
                dma((nt,)), dma((nt,)), dma, dma,
                dma((nt, nc)), dma((nt, nc)), dma((nt, nc)), dma((nt, nc)), dma((nt, nc)), dma((nt, nc)),
            ],
            compiler_params=pltpu.CompilerParams(collective_id=0, has_side_effects=True),
        )(pattern, coupling[0, 0], log_diag.reshape(nt, t), boundary)
        return result[None, None]

    return jax.shard_map(
        shards,
        mesh=mesh,
        in_specs=(P("outer", "inner", None, None, None), P("outer", "inner", None), P(), P()),
        out_specs=P("outer", "inner", None, None),
        check_vma=False,
    )
```
